32 devices in a mesh: fiber: 2 (over x), blk: 16 (over z, y, core).
Axes of the slice: x: 2, y: 2, z: 4, core: 2. Of those that a mesh axis runs over, the one named last changes fastest.
Arguments:
- users: bfloat16 [32768, 256], P('blk', 'fiber'), may hold values from -1.5 to 1.5
- items: bfloat16 [4096, 256], P('blk'), may hold values from -1.5 to 1.5
- tile_users: int32 [16, 2, 128], P('blk', 'fiber'), may hold values from 0 to 15
- tile_items: int32 [16, 2, 128], P('blk', 'fiber'), may hold values from 0 to 31, as said below
- confidence: bfloat16 [16, 2, 128, 128, 128], P('blk', 'fiber'), may hold values from 0.19921875 to 5
Outputs:
- user_grad: bfloat16 [32768, 256], P('blk', 'fiber')
The draws below stay inside these ranges and needn't reach their ends.
Inputs may be any that keep to these rules, and one draw needn't show every extreme that they name: `tile_items`: each device's list is sorted by item block, then user block, and holds distinct pairs; the two lists of the same index of blk share no pair. A device has at most 8 tiles in any item block, and exactly 8 in at least one.
All inputs are finite; a program needn't handle non-finite values.
Results may differ from the reference program's by a relative error of at most 0.0034.
Values may be sent and summed in bfloat16 or wider, within the bound.
No kernel may reach another device: no remote copies, remote signals or barrier semaphores. Data moves between devices by JAX's collectives and lax.ppermute only.
A program may use at most 128 MiB of HBM per device.

```python
import math
import jax
import jax.numpy as jnp
from jax import lax

R = 256
TB = 128
MOST = 8
UBD = 16
NIB = 32
TILES = 128
NU = 32768
NI = 4096
N_FIBER = 2
N_BLK = 16


def tile_lists(key):
    pairs = NIB * UBD

    def one_device(device_key):
        key_perm, key_bias, key_score, key_full = jax.random.split(device_key, 4)
        orders = jax.vmap(lambda k: jax.random.permutation(k, UBD))(jax.random.split(key_perm, NIB))
        picked = orders[:, :MOST * N_FIBER].reshape(NIB, N_FIBER, MOST).transpose(1, 0, 2).astype(jnp.int32)
        bias = jax.random.randint(key_bias, (N_FIBER, NIB), 0, 2 ** 16)
        full_block = jax.random.randint(key_full, (N_FIBER,), 0, NIB)
        bias = jnp.where(jnp.arange(NIB)[None, :] == full_block[:, None], 2 ** 17, bias)
        raw = jax.random.randint(key_score, (N_FIBER, NIB, MOST), 0, 2 ** 16)
        pair_ids = jnp.arange(NIB, dtype=jnp.int32)[None, :, None] * UBD + picked
        scores = ((raw + bias[:, :, None]) * pairs + pair_ids).reshape(N_FIBER, -1).astype(jnp.int32)
        best = lax.top_k(scores, TILES)[0]
        chosen = jnp.sort(best % pairs, axis=-1).astype(jnp.int32)
        return (chosen % UBD, chosen // UBD)
    device_keys = jax.random.split(jax.random.fold_in(key, 11), N_BLK)
    return jax.vmap(one_device)(device_keys)


def draw_tile_users(key, part):
    return tile_lists(key)[0].astype(jnp.int32)


def draw_tile_items(key, part):
    return tile_lists(key)[1].astype(jnp.int32)


def levels(rng, extent, cuts, smallest, high):
    level, own = 1.0, jax.random.fold_in(rng, 6)
    for dim, shards_of in cuts:
        heights = jnp.exp(jax.random.uniform(jax.random.fold_in(own, dim), (shards_of,), jnp.float32, smallest / len(cuts), high / len(cuts)))
        level = level * jnp.repeat(heights, extent[dim] // shards_of).reshape([-1 if axis == dim else 1 for axis in range(len(extent))])
    return level


def centred(key, extent, width, most, cuts=(), kind=jnp.bfloat16):
    factor_of = levels(key, extent, cuts, -0.22, 0.18) if cuts else 1.0
    values = jax.random.normal(key, extent, jnp.float32) * width * factor_of
    return jnp.minimum(jnp.maximum(values, -most), most).astype(kind)


def setup_inputs(seed: int = 0) -> dict:
    key_of = jax.random.split(jax.random.key(seed), 6)
    users = centred(key_of[0], (NU, R), 0.25, 1.5, ((0, 16), (1, 2)))
    items = centred(key_of[1], (NI, R), 0.25, 1.5, ((0, 16),))
    tile_users = draw_tile_users(jax.random.fold_in(key_of[5], 71), 0)
    tile_items = draw_tile_items(jax.random.fold_in(key_of[5], 71), 0)
    confidence = jnp.clip(jnp.exp(math.log(5.0) - 3.2227897 * jax.random.uniform(key_of[4], (N_BLK, N_FIBER, TILES, TB, TB), jnp.float32) ** levels(key_of[4], (N_BLK, N_FIBER, TILES, TB, TB), ((0, 16), (1, 2)), -0.2, 0.2)), 0.19921875, 5.0).astype(jnp.bfloat16)
    return {"users": users, "items": items, "tile_users": tile_users, "tile_items": tile_items, "confidence": confidence}


def reference(users, items, tile_users, tile_items, confidence):
    user_blocks = users.reshape(-1, TB, R)
    item_blocks = items.reshape(-1, TB, R)
    offsets = (jnp.arange(N_BLK, dtype=jnp.int32) * UBD)[:, None, None]
    list_users = (tile_users + offsets).astype(jnp.int32).reshape(-1, TILES)
    list_items = tile_items.reshape(-1, TILES)
    conf_lists = confidence.reshape(-1, TILES, TB, TB)

    def device_step(carry, inputs):
        totals, row_weight = carry
        user_ids, item_ids, conf_tiles = inputs
        user_rows = user_blocks[user_ids].astype(jnp.float32)
        item_rows = item_blocks[item_ids].astype(jnp.float32)
        scores = jnp.einsum('tar,tbr->tab', user_rows, item_rows, precision=lax.Precision.HIGHEST)
        weight = (conf_tiles.astype(jnp.float32) * (1.0 - scores)).astype(jnp.bfloat16)
        weight = lax.optimization_barrier(weight).astype(jnp.float32)
        products = jnp.einsum('tab,tbr->tar', weight, item_rows, precision=lax.Precision.HIGHEST)
        totals = totals.at[user_ids].add(products)
        row_weight = row_weight.at[user_ids].add(lax.optimization_barrier(jnp.sum(conf_tiles.astype(jnp.float32), axis=-1)))
        return ((totals, row_weight), None)
    start = (jnp.zeros((user_blocks.shape[0], TB, R), jnp.float32), jnp.ones((user_blocks.shape[0], TB), jnp.float32))
    (totals, row_weight), _ = lax.scan(device_step, start, (list_users, list_items, conf_lists))
    scaled = totals * lax.rsqrt(row_weight)[:, :, None]
    return scaled.reshape(-1, R).astype(jnp.bfloat16)
```

```python
import functools

import jax
import jax.numpy as jnp
from jax import lax
from jax.experimental import pallas as pl
from jax.experimental.pallas import tpu as pltpu
from jax.sharding import PartitionSpec as P


F32, BF16, I32 = jnp.float32, jnp.bfloat16, jnp.int32
VM = pl.BlockSpec(memory_space=pltpu.VMEM)
SM = pl.BlockSpec(memory_space=pltpu.SMEM)
STEP = 16
TILE_MIB = 16


def params(mib):
    return pltpu.CompilerParams(vmem_limit_bytes=mib << 20)


def is_late(slot, n_blk):
    return jnp.logical_and((slot & 2) != 0, (slot & (n_blk // 2)) != 0)


def lists(n_blk, per, blocks, users_ref, items_ref, tile_ref, block_ref, slot_ref, count_ref):
    tiles = users_ref.shape[0]
    base = tile_ref.shape[0] // 2
    me = lax.axis_index("blk").astype(I32)

    def body(i, carry):
        a, b = carry
        for j in range(8):
            t = i * 8 + j
            c = items_ref[t]
            slot = lax.div(c, per) ^ me
            hit = is_late(slot, n_blk)
            at = jnp.where(hit, base + b, a)
            tile_ref[at] = t
            block_ref[at] = users_ref[t]
            slot_ref[at] = slot * per + lax.rem(c, per)
            a, b = a + 1 - hit.astype(I32), b + hit.astype(I32)
        return a, b

    a, b = lax.fori_loop(0, tiles // 8, body, (0, 0))
    for start, spare in ((a, 0), (base + b, n_blk * per - 1)):
        for j in range(STEP):
            tile_ref[start + j] = 0
            block_ref[start + j] = blocks
            slot_ref[start + j] = spare
    count_ref[0] = lax.div(a + STEP - 1, STEP)
    count_ref[1] = lax.div(b + STEP - 1, STEP)
    count_ref[2] = lax.axis_index("fiber").astype(I32)


def row_sums(users_ref, conf_ref, mine_ref, items_ref, out_ref, mine_out, items_out, acc_ref):
    mine_out[...] = mine_ref[...]
    items_out[...] = items_ref[...]
    tiles, tb, _ = conf_ref.shape
    blocks = out_ref.shape[0]
    acc_ref[...] = jnp.zeros_like(acc_ref)

    def body(i, _):
        for j in range(4):
            acc_ref[users_ref[i * 4 + j]] += conf_ref[i * 4 + j].astype(F32)
        return 0

    lax.fori_loop(0, tiles // 4, body, 0)
    for k in range(blocks):
        out_ref[k] = jnp.broadcast_to(jnp.sum(acc_ref[k].T, axis=0, keepdims=True), (8, tb))


def scales(mine_ref, other_ref, out_ref):
    blocks, _, tb = mine_ref.shape
    for k in range(blocks):
        row = lax.rsqrt(1.0 + mine_ref[k] + other_ref[k])
        out_ref[k * tb : (k + 1) * tb, :] = jnp.broadcast_to(row[:1, :], (tb, tb)).T


def run_tiles(base, groups, tile_ref, block_ref, slot_ref, full_ref, item_ref, conf_ref, w_ref, acc_ref):
    tb = conf_ref.shape[1]
    last = full_ref.shape[0] // tb - 1

    def rows(block):
        return pl.ds(pl.multiple_of(block * tb, tb), tb)

    def body(g, _):
        first = base + g * STEP
        for j in range(STEP):
            u = full_ref[rows(jnp.minimum(block_ref[first + j], last)), :]
            v = item_ref[slot_ref[first + j]]
            s = lax.dot_general(u, v, (((1,), (1,)), ((), ())), preferred_element_type=F32)
            w_ref[j] = (conf_ref[tile_ref[first + j]].astype(F32) * (1.0 - s)).astype(BF16)
        for j in range(STEP):
            v = item_ref[slot_ref[first + j]]
            acc_ref[rows(block_ref[first + j]), :] += jnp.dot(w_ref[j], v, preferred_element_type=F32)
        return 0

    lax.fori_loop(0, groups, body, 0)


def fill(item_ref, slot_refs, places):
    tb = item_ref.shape[1]
    for s, ref in zip(places, slot_refs):
        per = ref.shape[0] // tb
        for j in range(per):
            item_ref[s * per + j] = ref[j * tb : (j + 1) * tb, :]


def early(places, count_ref, tile_ref, block_ref, slot_ref, mine_ref, other_ref, conf_ref, *refs):
    slot_refs = refs[: len(places)]
    full_ref, acc_ref, item_ref, w_ref = refs[len(places) :]
    half = mine_ref.shape[1]
    here = pl.multiple_of(count_ref[2] * half, half)
    there = pl.multiple_of((1 - count_ref[2]) * half, half)
    full_ref[:, pl.ds(here, half)] = mine_ref[...]
    full_ref[:, pl.ds(there, half)] = other_ref[...]
    fill(item_ref, slot_refs, places)
    acc_ref[...] = jnp.zeros_like(acc_ref)
    run_tiles(0, count_ref[0], tile_ref, block_ref, slot_ref, full_ref, item_ref, conf_ref, w_ref, acc_ref)


def late(places, count_ref, tile_ref, block_ref, slot_ref, full_ref, scale_ref, conf_ref, _, *refs):
    slot_refs = refs[: len(places)]
    keep_ref, send_ref, acc_ref, item_ref, w_ref = refs[len(places) :]
    rows, half = keep_ref.shape
    base = tile_ref.shape[0] // 2
    fill(item_ref, slot_refs, places)
    run_tiles(base, count_ref[1], tile_ref, block_ref, slot_ref, full_ref, item_ref, conf_ref, w_ref, acc_ref)
    here = pl.multiple_of(count_ref[2] * half, half)
    there = pl.multiple_of((1 - count_ref[2]) * half, half)
    send_ref[...] = (acc_ref[:rows, pl.ds(there, half)] * scale_ref[...]).astype(BF16)
    keep_ref[...] = acc_ref[:rows, pl.ds(here, half)] * scale_ref[...]


def gather_items(items, n_blk):
    def swap(x, bits):
        return lax.ppermute(x, "blk", [(i, i ^ bits) for i in range(n_blk)])

    got = {0: items, 2: swap(items, 2)}
    for d in range(4, n_blk, 4):
        low = d & -d
        got[d] = swap(items if d == low else got[d ^ low], d if d == low else low)
    for d in range(4, n_blk, 4):
        got[d | 2] = swap(got[d], 2)
    for d in range(0, n_blk, 2):
        got[d | 1] = swap(got[d], 1)
    return [got[d] for d in range(n_blk)]


def shards(users, items, tile_users, tile_items, confidence):
    n_fiber, n_blk = lax.axis_size("fiber"), lax.axis_size("blk")
    tb = confidence.shape[-1]
    rows, half = users.shape
    blocks = rows // tb
    per = items.shape[0] // tb
    user_list = tile_users.reshape(-1)
    item_list = tile_items.reshape(-1)
    conf = confidence.reshape(-1, tb, tb)
    tiles = conf.shape[0]
    swap_fiber = [(i, n_fiber - 1 - i) for i in range(n_fiber)]
    other = lax.ppermute(users, "fiber", swap_fiber)
    slots = gather_items(items, n_blk)
    entries = jax.ShapeDtypeStruct((2 * (tiles + STEP),), I32)
    tile, block, slot, count = pl.pallas_call(
        functools.partial(lists, n_blk, per, blocks),
        out_shape=(entries, entries, entries, jax.ShapeDtypeStruct((3,), I32)),
        in_specs=[SM, SM],
        out_specs=(SM, SM, SM, SM),
        compiler_params=params(2),
        cost_estimate=pl.CostEstimate(flops=0, bytes_accessed=conf.size * 4, transcendentals=0),
        name="lists",
    )(user_list, item_list)
    sums, mine, slots[0] = pl.pallas_call(
        row_sums,
        out_shape=(
            jax.ShapeDtypeStruct((blocks, 8, tb), F32),
            jax.ShapeDtypeStruct(users.shape, BF16),
            jax.ShapeDtypeStruct(items.shape, BF16),
        ),
        in_specs=[SM, VM, VM, VM],
        out_specs=(VM, VM, VM),
        scratch_shapes=[pltpu.VMEM((blocks, tb, tb), F32)],
        compiler_params=params(4),
        cost_estimate=pl.CostEstimate(flops=0, bytes_accessed=conf.size * 4, transcendentals=0),
        name="sums",
    )(user_list, conf, users, items)
    sums_other = lax.ppermute(sums, "fiber", swap_fiber)
    scale = pl.pallas_call(
        scales,
        out_shape=jax.ShapeDtypeStruct((rows, half), F32),
        in_specs=[VM, VM],
        out_specs=VM,
        compiler_params=params(2),
        name="scales",
    )(sums, sums_other)
    places = ([], [])
    for d in range(n_blk):
        places[bool(d & 2 and d & (n_blk // 2))].append(d)
    scratch = [pltpu.VMEM((n_blk * per, tb, 2 * half), BF16), pltpu.VMEM((STEP, tb, tb), BF16)]
    acc_shape = jax.ShapeDtypeStruct((rows + tb, 2 * half), F32)
    scalars = (count, tile, block, slot)
    full, acc = pl.pallas_call(
        functools.partial(early, places[0]),
        out_shape=(jax.ShapeDtypeStruct((rows, 2 * half), BF16), acc_shape),
        in_specs=[SM] * 4 + [VM] * (3 + len(places[0])),
        out_specs=(VM, VM),
        scratch_shapes=scratch,
        compiler_params=params(TILE_MIB),
        cost_estimate=pl.CostEstimate(flops=tiles * tb * tb * half * 8, bytes_accessed=0, transcendentals=0),
        name="early",
    )(*scalars, mine, other, conf, *[slots[d] for d in places[0]])
    keep, send, _ = pl.pallas_call(
        functools.partial(late, places[1]),
        out_shape=(jax.ShapeDtypeStruct((rows, half), F32), jax.ShapeDtypeStruct((rows, half), BF16), acc_shape),
        in_specs=[SM] * 4 + [VM] * (4 + len(places[1])),
        out_specs=(VM, VM, VM),
        scratch_shapes=scratch,
        input_output_aliases={7: 2},
        compiler_params=params(TILE_MIB),
        name="late",
    )(*scalars, full, scale, conf, acc, *[slots[d] for d in places[1]])
    arrived = lax.ppermute(send, "fiber", swap_fiber)
    return (keep + arrived.astype(F32)).astype(BF16)


def solution(mesh):
    in_specs = (
        P("blk", "fiber"),
        P("blk", None),
        P("blk", "fiber", None),
        P("blk", "fiber", None),
        P("blk", "fiber", None, None, None),
    )
    return jax.shard_map(shards, mesh=mesh, in_specs=in_specs, out_specs=P("blk", "fiber"), check_vma=False)
```

```python
import functools

import jax
import jax.numpy as jnp
from jax import lax
from jax.experimental import pallas as pl
from jax.experimental.pallas import tpu as pltpu
from jax.sharding import PartitionSpec as P


F32, BF16, I32 = jnp.float32, jnp.bfloat16, jnp.int32
VM = pl.BlockSpec(memory_space=pltpu.VMEM)
HBM = pl.BlockSpec(memory_space=pltpu.HBM)
SM = pl.BlockSpec(memory_space=pltpu.SMEM)
STEP = 16
UNROLL = 16
SLOT_BITS, BLOCK_BITS = 10, 8
TILE_MIB = 16


def params(mib):
    return pltpu.CompilerParams(vmem_limit_bytes=mib << 20)


def stage_of(slot, n_blk):
    chip = slot >> 1
    one = (chip & (chip - 1)) == 0
    return jnp.where(one, 0, jnp.where(chip == n_blk // 2 - 1, 2, 1))


def prepare(n_blk, per, spare, users_hbm, items_hbm, conf_hbm, mine_hbm, own_hbm, sums_ref, conf_ref, mine_ref, own_ref, list_ref, count_ref, users_ref, items_ref, table_ref, ends_ref, acc_ref, sems):
    tiles, _, _ = conf_ref.shape
    blocks = sums_ref.shape[0]
    parts = sems.shape[0] - 4
    part = tiles // parts
    base = list_ref.shape[0] // 4
    me = lax.axis_index("blk").astype(I32)

    def conf_copy(i):
        at = pl.ds(i * part, part)
        return pltpu.make_async_copy(conf_hbm.at[at], conf_ref.at[at], sems.at[i])

    def other_copy(src, dst, i):
        return pltpu.make_async_copy(src, dst, sems.at[parts + i])

    first = [other_copy(users_hbm, users_ref, 0), other_copy(items_hbm, items_ref, 1)]
    later = [other_copy(mine_hbm, mine_ref, 2), other_copy(own_hbm, own_ref, 3)]
    for c in first:
        c.start()
    for i in range(parts):
        conf_copy(i).start()
    for c in later:
        c.start()
    acc_ref[...] = jnp.zeros_like(acc_ref)
    for item in range(table_ref.shape[0]):
        slot = item // per ^ me
        table_ref[item] = (stage_of(slot, n_blk) << SLOT_BITS) + slot * per + item % per
    for i in range(4):
        ends_ref[i] = i * base
    for c in first:
        c.wait()

    def body(i, _):
        conf_copy(i).wait()

        def inner(j, _):
            for k in range(UNROLL):
                t = i * part + j * UNROLL + k
                user, found = users_ref[t], table_ref[items_ref[t]]
                stage = jnp.where(user >= blocks // 2, 3, found >> SLOT_BITS)
                end = ends_ref[stage]
                ends_ref[stage] = end + 1
                list_ref[end] = ((t << BLOCK_BITS) + user << SLOT_BITS) + (found & ((1 << SLOT_BITS) - 1))
                acc_ref[user] += conf_ref[t].astype(F32)
            return 0

        return lax.fori_loop(0, part // UNROLL, inner, 0)

    lax.fori_loop(0, parts, body, 0)
    ends = [ends_ref[i] for i in range(4)]
    spares = ((blocks // 2, 0), (blocks // 2, spare * per), (blocks // 2, n_blk * per - 1), (blocks, 0))
    for i, (end, (block, slot)) in enumerate(zip(ends, spares)):
        for j in range(STEP):
            list_ref[end + j] = (block << SLOT_BITS) + slot
        count_ref[i] = lax.div(end - i * base + STEP - 1, STEP)
    count_ref[4] = lax.axis_index("fiber").astype(I32)
    for k in range(blocks):
        sums_ref[k : k + 1, :] = jnp.sum(acc_ref[k].T, axis=0, keepdims=True)
    for c in later:
        c.wait()


def scales(mine_ref, other_ref, out_ref):
    blocks, tb = mine_ref.shape
    for k in range(blocks):
        row = lax.rsqrt(1.0 + mine_ref[k : k + 1, :] + other_ref[k : k + 1, :])
        out_ref[k * tb : (k + 1) * tb, :] = jnp.broadcast_to(row, (tb, tb)).T


def run_tiles(base, groups, first_block, list_ref, full_ref, item_ref, conf_ref, w_ref, acc_ref):
    tb = conf_ref.shape[1]
    blocks = full_ref.shape[0] // tb

    def rows(block):
        return pl.ds(pl.multiple_of(block * tb, tb), tb)

    def body(g, _):
        first = base + g * STEP
        entries = []
        for j in range(STEP):
            e = list_ref[first + j]
            block = (e >> SLOT_BITS) & ((1 << BLOCK_BITS) - 1)
            entries.append((e >> (SLOT_BITS + BLOCK_BITS), block, e & ((1 << SLOT_BITS) - 1)))
        for j, (tile, block, slot) in enumerate(entries):
            u = full_ref[rows(jnp.minimum(block, blocks - 1)), :]
            s = lax.dot_general(u, item_ref[slot], (((1,), (1,)), ((), ())), preferred_element_type=F32)
            w_ref[j] = (conf_ref[tile].astype(F32) * (1.0 - s)).astype(BF16)
        for j, (_, block, slot) in enumerate(entries):
            acc_ref[rows(block - first_block), :] += jnp.dot(w_ref[j], item_ref[slot], preferred_element_type=F32)
        return 0

    lax.fori_loop(0, groups, body, 0)


def fill(item_ref, slot_refs, places):
    tb = item_ref.shape[1]
    for s, ref in zip(places, slot_refs):
        per = ref.shape[0] // tb
        for j in range(per):
            item_ref[s * per + j] = ref[j * tb : (j + 1) * tb, :]


def early(places, count_ref, list_ref, mine_ref, other_ref, conf_ref, *refs):
    slot_refs = refs[: len(places)]
    full_ref, acc_ref, item_ref, w_ref = refs[len(places) :]
    half = mine_ref.shape[1]
    here = pl.multiple_of(count_ref[4] * half, half)
    there = pl.multiple_of((1 - count_ref[4]) * half, half)
    full_ref[:, pl.ds(here, half)] = mine_ref[...]
    full_ref[:, pl.ds(there, half)] = other_ref[...]
    fill(item_ref, slot_refs, places)
    acc_ref[...] = jnp.zeros_like(acc_ref)
    run_tiles(0, count_ref[0], 0, list_ref, full_ref, item_ref, conf_ref, w_ref, acc_ref)


def finish(keep_ref, send_ref, acc_ref, scale_ref, fiber, first):
    rows, half = keep_ref.shape
    here = pl.multiple_of(fiber * half, half)
    there = pl.multiple_of((1 - fiber) * half, half)
    scale = scale_ref[first : first + rows, :]
    send_ref[...] = (acc_ref[:rows, pl.ds(there, half)] * scale).astype(BF16)
    keep_ref[...] = acc_ref[:rows, pl.ds(here, half)] * scale


def middle(places, count_ref, list_ref, full_ref, conf_ref, _, *refs):
    slot_refs = refs[: len(places)]
    acc_ref, item_ref, w_ref = refs[len(places) :]
    base = list_ref.shape[0] // 4
    fill(item_ref, slot_refs, places)
    run_tiles(base, count_ref[1], 0, list_ref, full_ref, item_ref, conf_ref, w_ref, acc_ref)


def late(places, count_ref, list_ref, full_ref, scale_ref, conf_ref, _, *refs):
    slot_refs = refs[: len(places)]
    keep_ref, send_ref, acc_ref, item_ref, w_ref = refs[len(places) :]
    base = list_ref.shape[0] // 4
    fill(item_ref, slot_refs, places)
    run_tiles(2 * base, count_ref[2], 0, list_ref, full_ref, item_ref, conf_ref, w_ref, acc_ref)
    finish(keep_ref, send_ref, acc_ref, scale_ref, count_ref[4], 0)


def second(places, count_ref, list_ref, full_ref, scale_ref, conf_ref, _, *refs):
    slot_refs = refs[: len(places)]
    keep_ref, send_ref, acc_ref, item_ref, w_ref = refs[len(places) :]
    rows = keep_ref.shape[0]
    base = list_ref.shape[0] // 4
    fill(item_ref, slot_refs, places)
    acc_ref[...] = jnp.zeros_like(acc_ref)
    block = rows // conf_ref.shape[1]
    run_tiles(3 * base, count_ref[3], block, list_ref, full_ref, item_ref, conf_ref, w_ref, acc_ref)
    finish(keep_ref, send_ref, acc_ref, scale_ref, count_ref[4], rows)


def gather_items(items, n_blk):
    def swap(x, bits):
        return lax.ppermute(x, "blk", [(i, i ^ bits) for i in range(n_blk)])

    got = {0: items, 2: swap(items, 2)}
    for d in range(4, n_blk, 4):
        low = d & -d
        got[d] = swap(items if d == low else got[d ^ low], d if d == low else low)
    for d in range(4, n_blk, 4):
        got[d | 2] = swap(got[d], 2)
    for d in range(0, n_blk, 2):
        got[d | 1] = swap(got[d], 1)
    return [got[d] for d in range(n_blk)]


def shards(users, items, tile_users, tile_items, confidence):
    n_fiber, n_blk = lax.axis_size("fiber"), lax.axis_size("blk")
    tb = confidence.shape[-1]
    rows, half = users.shape
    blocks = rows // tb
    per = items.shape[0] // tb
    user_list = tile_users.reshape(-1)
    item_list = tile_items.reshape(-1)
    conf = confidence.reshape(-1, tb, tb)
    tiles = conf.shape[0]
    swap_fiber = [(i, n_fiber - 1 - i) for i in range(n_fiber)]
    other = lax.ppermute(users, "fiber", swap_fiber)
    slots = gather_items(items, n_blk)
    places = ([], [], [])
    for d in range(n_blk):
        chip = d >> 1
        places[0 if chip & (chip - 1) == 0 else 2 if chip == n_blk // 2 - 1 else 1].append(d)
    hbm = [pltpu.with_memory_space_constraint(x, pltpu.HBM) for x in (user_list, item_list, conf, users, items)]
    sums, conf_v, mine, slots[0], order, count = pl.pallas_call(
        functools.partial(prepare, n_blk, per, places[1][0]),
        out_shape=(
            jax.ShapeDtypeStruct((blocks, tb), F32),
            jax.ShapeDtypeStruct(conf.shape, BF16),
            jax.ShapeDtypeStruct(users.shape, BF16),
            jax.ShapeDtypeStruct(items.shape, BF16),
            jax.ShapeDtypeStruct((4 * (tiles + STEP),), I32),
            jax.ShapeDtypeStruct((5,), I32),
        ),
        in_specs=[HBM] * 5,
        out_specs=(VM, VM, VM, VM, SM, SM),
        scratch_shapes=[
            pltpu.SMEM((tiles,), I32),
            pltpu.SMEM((tiles,), I32),
            pltpu.SMEM((n_blk * per,), I32),
            pltpu.SMEM((4,), I32),
            pltpu.VMEM((blocks, tb, tb), F32),
            pltpu.SemaphoreType.DMA((8 + 4,)),
        ],
        compiler_params=params(4),
        cost_estimate=pl.CostEstimate(flops=0, bytes_accessed=conf.size * 4, transcendentals=0),
        name="prepare",
    )(*hbm)
    sums_other = lax.ppermute(sums, "fiber", swap_fiber)
    scale = pl.pallas_call(
        scales,
        out_shape=jax.ShapeDtypeStruct((rows, half), F32),
        in_specs=[VM, VM],
        out_specs=VM,
        compiler_params=params(2),
        name="scales",
    )(sums, sums_other)
    scratch = [pltpu.VMEM((n_blk * per, tb, 2 * half), BF16), pltpu.VMEM((STEP, tb, tb), BF16)]
    acc_shape = jax.ShapeDtypeStruct((rows // 2 + tb, 2 * half), F32)
    half_shapes = (jax.ShapeDtypeStruct((rows // 2, half), F32), jax.ShapeDtypeStruct((rows // 2, half), BF16))
    scalars = (count, order)
    full, acc = pl.pallas_call(
        functools.partial(early, places[0]),
        out_shape=(jax.ShapeDtypeStruct((rows, 2 * half), BF16), acc_shape),
        in_specs=[SM] * 2 + [VM] * (3 + len(places[0])),
        out_specs=(VM, VM),
        scratch_shapes=scratch,
        compiler_params=params(TILE_MIB),
        cost_estimate=pl.CostEstimate(flops=tiles * tb * tb * half * 8, bytes_accessed=0, transcendentals=0),
        name="early",
    )(*scalars, mine, other, conf_v, *[slots[d] for d in places[0]])
    acc = pl.pallas_call(
        functools.partial(middle, places[1]),
        out_shape=acc_shape,
        in_specs=[SM] * 2 + [VM] * (3 + len(places[1])),
        out_specs=VM,
        scratch_shapes=scratch,
        input_output_aliases={4: 0},
        compiler_params=params(TILE_MIB),
        cost_estimate=pl.CostEstimate(flops=tiles * tb * tb * half * 4, bytes_accessed=0, transcendentals=0),
        name="middle",
    )(*scalars, full, conf_v, acc, *[slots[d] for d in places[1]])
    keep, send, _ = pl.pallas_call(
        functools.partial(late, places[2]),
        out_shape=(*half_shapes, acc_shape),
        in_specs=[SM] * 2 + [VM] * (4 + len(places[2])),
        out_specs=(VM, VM, VM),
        scratch_shapes=scratch,
        input_output_aliases={5: 2},
        compiler_params=params(TILE_MIB),
        cost_estimate=pl.CostEstimate(flops=tiles * tb * tb * half * 8, bytes_accessed=0, transcendentals=0),
        name="late",
    )(*scalars, full, scale, conf_v, acc, *[slots[d] for d in places[2]])
    arrived = lax.ppermute(send, "fiber", swap_fiber)
    keep2, send2 = pl.pallas_call(
        functools.partial(second, range(n_blk)),
        out_shape=half_shapes,
        in_specs=[SM] * 2 + [VM] * (4 + n_blk),
        out_specs=(VM, VM),
        scratch_shapes=[pltpu.VMEM(acc_shape.shape, F32)] + scratch,
        compiler_params=params(TILE_MIB),
        cost_estimate=pl.CostEstimate(flops=tiles * tb * tb * half * 8, bytes_accessed=0, transcendentals=0),
        name="second",
    )(*scalars, full, scale, conf_v, keep, *slots)
    arrived2 = lax.ppermute(send2, "fiber", swap_fiber)
    return jnp.concatenate([(keep + arrived.astype(F32)).astype(BF16), (keep2 + arrived2.astype(F32)).astype(BF16)])


def solution(mesh):
    in_specs = (
        P("blk", "fiber"),
        P("blk", None),
        P("blk", "fiber", None),
        P("blk", "fiber", None),
        P("blk", "fiber", None, None, None),
    )
    return jax.shard_map(shards, mesh=mesh, in_specs=in_specs, out_specs=P("blk", "fiber"), check_vma=False)
```

```python
import functools

import jax
import jax.numpy as jnp
from jax import lax
from jax.experimental import pallas as pl
from jax.experimental.pallas import tpu as pltpu
from jax.sharding import PartitionSpec as P


F32, BF16, I32 = jnp.float32, jnp.bfloat16, jnp.int32
VM = pl.BlockSpec(memory_space=pltpu.VMEM)
HBM = pl.BlockSpec(memory_space=pltpu.HBM)
SM = pl.BlockSpec(memory_space=pltpu.SMEM)
STEP = 16
UNROLL = 16
SLOT_BITS, BLOCK_BITS = 10, 8
TILE_MIB = 16


def params(mib):
    return pltpu.CompilerParams(vmem_limit_bytes=mib << 20)


def stage_of(slot, n_blk):
    chip = slot >> 1
    one = (chip & (chip - 1)) == 0
    return jnp.where(one, 0, jnp.where(chip == n_blk // 2 - 1, 2, 1))


def prepare(n_blk, per, spare, users_hbm, items_hbm, conf_hbm, mine_hbm, own_hbm, sums_ref, conf_ref, mine_ref, own_ref, list_ref, count_ref, users_ref, items_ref, table_ref, ends_ref, acc_ref, sems):
    tiles, _, _ = conf_ref.shape
    blocks = sums_ref.shape[0]
    parts = sems.shape[0] - 4
    part = tiles // parts
    base = list_ref.shape[0] // 4
    me = lax.axis_index("blk").astype(I32)

    def conf_copy(i):
        at = pl.ds(i * part, part)
        return pltpu.make_async_copy(conf_hbm.at[at], conf_ref.at[at], sems.at[i])

    def other_copy(src, dst, i):
        return pltpu.make_async_copy(src, dst, sems.at[parts + i])

    first = [other_copy(users_hbm, users_ref, 0), other_copy(items_hbm, items_ref, 1)]
    later = [other_copy(mine_hbm, mine_ref, 2), other_copy(own_hbm, own_ref, 3)]
    for c in first:
        c.start()
    for i in range(parts):
        conf_copy(i).start()
    for c in later:
        c.start()
    acc_ref[...] = jnp.zeros_like(acc_ref)
    for item in range(table_ref.shape[0]):
        slot = item // per ^ me
        table_ref[item] = (stage_of(slot, n_blk) << SLOT_BITS) + slot * per + item % per
    for i in range(4):
        ends_ref[i] = i * base
    for c in first:
        c.wait()

    def body(i, _):
        conf_copy(i).wait()

        def inner(j, _):
            for k in range(UNROLL):
                t = i * part + j * UNROLL + k
                user, found = users_ref[t], table_ref[items_ref[t]]
                stage = jnp.where(user >= blocks // 2, 3, found >> SLOT_BITS)
                end = ends_ref[stage]
                ends_ref[stage] = end + 1
                list_ref[end] = ((t << BLOCK_BITS) + user << SLOT_BITS) + (found & ((1 << SLOT_BITS) - 1))
                acc_ref[user] += conf_ref[t].astype(F32)
            return 0

        return lax.fori_loop(0, part // UNROLL, inner, 0)

    lax.fori_loop(0, parts, body, 0)
    ends = [ends_ref[i] for i in range(4)]
    spares = ((blocks // 2, 0), (blocks // 2, spare * per), (blocks // 2, n_blk * per - 1), (blocks, 0))
    for i, (end, (block, slot)) in enumerate(zip(ends, spares)):
        for j in range(STEP):
            list_ref[end + j] = (block << SLOT_BITS) + slot
        count_ref[i] = lax.div(end - i * base + STEP - 1, STEP)
    count_ref[4] = lax.axis_index("fiber").astype(I32)
    for k in range(blocks):
        sums_ref[k : k + 1, :] = jnp.sum(acc_ref[k].T, axis=0, keepdims=True)
    for c in later:
        c.wait()


def scales(mine_ref, other_ref, out_ref):
    blocks, tb = mine_ref.shape
    for k in range(blocks):
        row = lax.rsqrt(1.0 + mine_ref[k : k + 1, :] + other_ref[k : k + 1, :])
        out_ref[k * tb : (k + 1) * tb, :] = jnp.broadcast_to(row, (tb, tb)).T


def run_tiles(base, groups, first_block, list_ref, full_ref, item_ref, conf_ref, w_ref, acc_ref):
    tb = conf_ref.shape[1]
    blocks = full_ref.shape[0] // tb

    def rows(block):
        return pl.ds(pl.multiple_of(block * tb, tb), tb)

    def body(g, _):
        first = base + g * STEP
        entries = []
        for j in range(STEP):
            e = list_ref[first + j]
            block = (e >> SLOT_BITS) & ((1 << BLOCK_BITS) - 1)
            entries.append((e >> (SLOT_BITS + BLOCK_BITS), block, e & ((1 << SLOT_BITS) - 1)))
        for j, (tile, block, slot) in enumerate(entries):
            u = full_ref[rows(jnp.minimum(block, blocks - 1)), :]
            s = lax.dot_general(u, item_ref[slot], (((1,), (1,)), ((), ())), preferred_element_type=F32)
            w_ref[j] = (conf_ref[tile].astype(F32) * (1.0 - s)).astype(BF16)
        for j, (_, block, slot) in enumerate(entries):
            acc_ref[rows(block - first_block), :] += jnp.dot(w_ref[j], item_ref[slot], preferred_element_type=F32)
        return 0

    lax.fori_loop(0, groups, body, 0)


def fill(item_ref, slot_refs, places):
    tb = item_ref.shape[1]
    for s, ref in zip(places, slot_refs):
        per = ref.shape[0] // tb
        for j in range(per):
            item_ref[s * per + j] = ref[j * tb : (j + 1) * tb, :]


def early(places, count_ref, list_ref, mine_ref, other_ref, conf_ref, *refs):
    slot_refs = refs[: len(places)]
    full_ref, acc_ref, item_ref, w_ref = refs[len(places) :]
    half = mine_ref.shape[1]
    here = pl.multiple_of(count_ref[4] * half, half)
    there = pl.multiple_of((1 - count_ref[4]) * half, half)
    full_ref[:, pl.ds(here, half)] = mine_ref[...]
    full_ref[:, pl.ds(there, half)] = other_ref[...]
    fill(item_ref, slot_refs, places)
    acc_ref[...] = jnp.zeros_like(acc_ref)
    run_tiles(0, count_ref[0], 0, list_ref, full_ref, item_ref, conf_ref, w_ref, acc_ref)


def finish(keep_ref, send_ref, acc_ref, scale_ref, fiber, first):
    rows, half = keep_ref.shape
    here = pl.multiple_of(fiber * half, half)
    there = pl.multiple_of((1 - fiber) * half, half)
    scale = scale_ref[first : first + rows, :]
    send_ref[...] = (acc_ref[:rows, pl.ds(there, half)] * scale).astype(BF16)
    keep_ref[...] = acc_ref[:rows, pl.ds(here, half)] * scale


def middle(places, count_ref, list_ref, full_ref, conf_ref, _, *refs):
    slot_refs = refs[: len(places)]
    acc_ref, item_ref, w_ref = refs[len(places) :]
    base = list_ref.shape[0] // 4
    fill(item_ref, slot_refs, places)
    run_tiles(base, count_ref[1], 0, list_ref, full_ref, item_ref, conf_ref, w_ref, acc_ref)


def late(places, count_ref, list_ref, full_ref, scale_ref, conf_ref, _, *refs):
    slot_refs = refs[: len(places)]
    keep_ref, send_ref, acc_ref, item_ref, w_ref = refs[len(places) :]
    base = list_ref.shape[0] // 4
    fill(item_ref, slot_refs, places)
    run_tiles(2 * base, count_ref[2], 0, list_ref, full_ref, item_ref, conf_ref, w_ref, acc_ref)
    finish(keep_ref, send_ref, acc_ref, scale_ref, count_ref[4], 0)


def second(places, count_ref, list_ref, full_ref, scale_ref, conf_ref, _, *refs):
    slot_refs = refs[: len(places)]
    keep_ref, send_ref, acc_ref, item_ref, w_ref = refs[len(places) :]
    rows = keep_ref.shape[0]
    base = list_ref.shape[0] // 4
    fill(item_ref, slot_refs, places)
    acc_ref[...] = jnp.zeros_like(acc_ref)
    block = rows // conf_ref.shape[1]
    run_tiles(3 * base, count_ref[3], block, list_ref, full_ref, item_ref, conf_ref, w_ref, acc_ref)
    finish(keep_ref, send_ref, acc_ref, scale_ref, count_ref[4], rows)


def write(part, keep_ref, came_ref, *refs):
    out_ref, buf, sems = refs[-3:]
    rows = keep_ref.shape[0]
    piece = rows // 2
    copies = []
    for i in range(2):
        at = pl.ds(i * piece, piece)
        buf[at, :] = (keep_ref[at, :] + came_ref[at, :].astype(F32)).astype(BF16)
        copies.append(pltpu.make_async_copy(buf.at[at], out_ref.at[pl.ds(part * rows + i * piece, piece)], sems.at[i]))
        copies[-1].start()
    for c in copies:
        c.wait()


def gather_items(items, n_blk):
    def swap(x, bits):
        return lax.ppermute(x, "blk", [(i, i ^ bits) for i in range(n_blk)])

    got = {0: items, 2: swap(items, 2)}
    for d in range(4, n_blk, 4):
        low = d & -d
        got[d] = swap(items if d == low else got[d ^ low], d if d == low else low)
    for d in range(4, n_blk, 4):
        got[d | 2] = swap(got[d], 2)
    for d in range(0, n_blk, 2):
        got[d | 1] = swap(got[d], 1)
    return [got[d] for d in range(n_blk)]


def shards(users, items, tile_users, tile_items, confidence):
    n_fiber, n_blk = lax.axis_size("fiber"), lax.axis_size("blk")
    tb = confidence.shape[-1]
    rows, half = users.shape
    blocks = rows // tb
    per = items.shape[0] // tb
    user_list = tile_users.reshape(-1)
    item_list = tile_items.reshape(-1)
    conf = confidence.reshape(-1, tb, tb)
    tiles = conf.shape[0]
    swap_fiber = [(i, n_fiber - 1 - i) for i in range(n_fiber)]
    other = lax.ppermute(users, "fiber", swap_fiber)
    slots = gather_items(items, n_blk)
    places = ([], [], [])
    for d in range(n_blk):
        chip = d >> 1
        places[0 if chip & (chip - 1) == 0 else 2 if chip == n_blk // 2 - 1 else 1].append(d)
    hbm = [pltpu.with_memory_space_constraint(x, pltpu.HBM) for x in (user_list, item_list, conf, users, items)]
    sums, conf_v, mine, slots[0], order, count = pl.pallas_call(
        functools.partial(prepare, n_blk, per, places[1][0]),
        out_shape=(
            jax.ShapeDtypeStruct((blocks, tb), F32),
            jax.ShapeDtypeStruct(conf.shape, BF16),
            jax.ShapeDtypeStruct(users.shape, BF16),
            jax.ShapeDtypeStruct(items.shape, BF16),
            jax.ShapeDtypeStruct((4 * (tiles + STEP),), I32),
            jax.ShapeDtypeStruct((5,), I32),
        ),
        in_specs=[HBM] * 5,
        out_specs=(VM, VM, VM, VM, SM, SM),
        scratch_shapes=[
            pltpu.SMEM((tiles,), I32),
            pltpu.SMEM((tiles,), I32),
            pltpu.SMEM((n_blk * per,), I32),
            pltpu.SMEM((4,), I32),
            pltpu.VMEM((blocks, tb, tb), F32),
            pltpu.SemaphoreType.DMA((8 + 4,)),
        ],
        compiler_params=params(4),
        cost_estimate=pl.CostEstimate(flops=0, bytes_accessed=conf.size * 4, transcendentals=0),
        name="prepare",
    )(*hbm)
    sums_other = lax.ppermute(sums, "fiber", swap_fiber)
    scale = pl.pallas_call(
        scales,
        out_shape=jax.ShapeDtypeStruct((rows, half), F32),
        in_specs=[VM, VM],
        out_specs=VM,
        compiler_params=params(2),
        name="scales",
    )(sums, sums_other)
    scratch = [pltpu.VMEM((n_blk * per, tb, 2 * half), BF16), pltpu.VMEM((STEP, tb, tb), BF16)]
    acc_shape = jax.ShapeDtypeStruct((rows // 2 + tb, 2 * half), F32)
    half_shapes = (jax.ShapeDtypeStruct((rows // 2, half), F32), jax.ShapeDtypeStruct((rows // 2, half), BF16))
    scalars = (count, order)
    full, acc = pl.pallas_call(
        functools.partial(early, places[0]),
        out_shape=(jax.ShapeDtypeStruct((rows, 2 * half), BF16), acc_shape),
        in_specs=[SM] * 2 + [VM] * (3 + len(places[0])),
        out_specs=(VM, VM),
        scratch_shapes=scratch,
        compiler_params=params(TILE_MIB),
        cost_estimate=pl.CostEstimate(flops=tiles * tb * tb * half * 8, bytes_accessed=0, transcendentals=0),
        name="early",
    )(*scalars, mine, other, conf_v, *[slots[d] for d in places[0]])
    acc = pl.pallas_call(
        functools.partial(middle, places[1]),
        out_shape=acc_shape,
        in_specs=[SM] * 2 + [VM] * (3 + len(places[1])),
        out_specs=VM,
        scratch_shapes=scratch,
        input_output_aliases={4: 0},
        compiler_params=params(TILE_MIB),
        cost_estimate=pl.CostEstimate(flops=tiles * tb * tb * half * 4, bytes_accessed=0, transcendentals=0),
        name="middle",
    )(*scalars, full, conf_v, acc, *[slots[d] for d in places[1]])
    keep, send, _ = pl.pallas_call(
        functools.partial(late, places[2]),
        out_shape=(*half_shapes, acc_shape),
        in_specs=[SM] * 2 + [VM] * (4 + len(places[2])),
        out_specs=(VM, VM, VM),
        scratch_shapes=scratch,
        input_output_aliases={5: 2},
        compiler_params=params(TILE_MIB),
        cost_estimate=pl.CostEstimate(flops=tiles * tb * tb * half * 8, bytes_accessed=0, transcendentals=0),
        name="late",
    )(*scalars, full, scale, conf_v, acc, *[slots[d] for d in places[2]])
    arrived = lax.ppermute(send, "fiber", swap_fiber)
    keep2, send2 = pl.pallas_call(
        functools.partial(second, range(n_blk)),
        out_shape=half_shapes,
        in_specs=[SM] * 2 + [VM] * (4 + n_blk),
        out_specs=(VM, VM),
        scratch_shapes=[pltpu.VMEM(acc_shape.shape, F32)] + scratch,
        compiler_params=params(TILE_MIB),
        cost_estimate=pl.CostEstimate(flops=tiles * tb * tb * half * 8, bytes_accessed=0, transcendentals=0),
        name="second",
    )(*scalars, full, scale, conf_v, keep, *slots)
    arrived2 = lax.ppermute(send2, "fiber", swap_fiber)
    out = None
    for i, (kept, came) in enumerate(((keep, arrived), (keep2, arrived2))):
        out = pl.pallas_call(
            functools.partial(write, i),
            out_shape=pltpu.HBM(users.shape, BF16),
            in_specs=[VM, VM] + [HBM] * i,
            out_specs=HBM,
            scratch_shapes=[pltpu.VMEM(came.shape, BF16), pltpu.SemaphoreType.DMA((2,))],
            input_output_aliases={2: 0} if i else {},
            compiler_params=params(2),
        )(kept, came, *([out] if i else []))
    return out


def solution(mesh):
    in_specs = (
        P("blk", "fiber"),
        P("blk", None),
        P("blk", "fiber", None),
        P("blk", "fiber", None),
        P("blk", "fiber", None, None, None),
    )
    return jax.shard_map(shards, mesh=mesh, in_specs=in_specs, out_specs=P("blk", "fiber"), check_vma=False)
```

```python
import functools

import jax
import jax.numpy as jnp
from jax import lax
from jax.experimental import pallas as pl
from jax.experimental.pallas import tpu as pltpu
from jax.sharding import PartitionSpec as P


F32, BF16, I32 = jnp.float32, jnp.bfloat16, jnp.int32
VM = pl.BlockSpec(memory_space=pltpu.VMEM)
HBM = pl.BlockSpec(memory_space=pltpu.HBM)
SM = pl.BlockSpec(memory_space=pltpu.SMEM)
STEP = 16
UNROLL = 16
SLOT_BITS, BLOCK_BITS = 10, 8
TILE_MIB = 16


def params(mib):
    return pltpu.CompilerParams(vmem_limit_bytes=mib << 20)


def stage_of(slot, n_blk):
    chip = slot >> 1
    one = (chip & (chip - 1)) == 0
    return jnp.where(one, 0, jnp.where(chip == n_blk // 2 - 1, 2, 1))


def prepare(n_blk, per, spare, users_hbm, items_hbm, conf_hbm, mine_hbm, own_hbm, sums_ref, conf_ref, mine_ref, own_ref, list_ref, count_ref, zero1_ref, zero2_ref, users_ref, items_ref, table_ref, ends_ref, acc_ref, sems):
    tiles, _, _ = conf_ref.shape
    blocks = sums_ref.shape[0]
    parts = sems.shape[0] - 4
    part = tiles // parts
    base = list_ref.shape[0] // 4
    me = lax.axis_index("blk").astype(I32)

    def conf_copy(i):
        at = pl.ds(i * part, part)
        return pltpu.make_async_copy(conf_hbm.at[at], conf_ref.at[at], sems.at[i])

    def other_copy(src, dst, i):
        return pltpu.make_async_copy(src, dst, sems.at[parts + i])

    first = [other_copy(users_hbm, users_ref, 0), other_copy(items_hbm, items_ref, 1)]
    later = [other_copy(mine_hbm, mine_ref, 2), other_copy(own_hbm, own_ref, 3)]
    for c in first:
        c.start()
    for i in range(parts):
        conf_copy(i).start()
    for c in later:
        c.start()
    for ref in (acc_ref, zero1_ref, zero2_ref):
        ref[...] = jnp.zeros_like(ref)
    for item in range(table_ref.shape[0]):
        slot = item // per ^ me
        table_ref[item] = (stage_of(slot, n_blk) << SLOT_BITS) + slot * per + item % per
    for i in range(4):
        ends_ref[i] = i * base
    for c in first:
        c.wait()

    def body(i, _):
        conf_copy(i).wait()

        def inner(j, _):
            for k in range(UNROLL):
                t = i * part + j * UNROLL + k
                user, found = users_ref[t], table_ref[items_ref[t]]
                stage = jnp.where(user >= blocks // 2, 3, found >> SLOT_BITS)
                end = ends_ref[stage]
                ends_ref[stage] = end + 1
                list_ref[end] = ((t << BLOCK_BITS) + user << SLOT_BITS) + (found & ((1 << SLOT_BITS) - 1))
                acc_ref[user] += conf_ref[t].astype(F32)
            return 0

        return lax.fori_loop(0, part // UNROLL, inner, 0)

    lax.fori_loop(0, parts, body, 0)
    ends = [ends_ref[i] for i in range(4)]
    spares = ((blocks // 2, 0), (blocks // 2, spare * per), (blocks // 2, n_blk * per - 1), (blocks, 0))
    for i, (end, (block, slot)) in enumerate(zip(ends, spares)):
        for j in range(STEP):
            list_ref[end + j] = (block << SLOT_BITS) + slot
        count_ref[i] = lax.div(end - i * base + STEP - 1, STEP)
    count_ref[4] = lax.axis_index("fiber").astype(I32)
    for k in range(blocks):
        sums_ref[k : k + 1, :] = jnp.sum(acc_ref[k].T, axis=0, keepdims=True)
    for c in later:
        c.wait()


def scales(mine_ref, other_ref, out_ref):
    blocks, tb = mine_ref.shape
    for k in range(blocks):
        row = lax.rsqrt(1.0 + mine_ref[k : k + 1, :] + other_ref[k : k + 1, :])
        out_ref[k * tb : (k + 1) * tb, :] = jnp.broadcast_to(row, (tb, tb)).T


def run_tiles(base, groups, first_block, list_ref, full_ref, item_ref, conf_ref, w_ref, acc_ref):
    tb = conf_ref.shape[1]
    blocks = full_ref.shape[0] // tb

    def rows(block):
        return pl.ds(pl.multiple_of(block * tb, tb), tb)

    def body(g, _):
        first = base + g * STEP
        entries = []
        for j in range(STEP):
            e = list_ref[first + j]
            block = (e >> SLOT_BITS) & ((1 << BLOCK_BITS) - 1)
            entries.append((e >> (SLOT_BITS + BLOCK_BITS), block, e & ((1 << SLOT_BITS) - 1)))
        for j, (tile, block, slot) in enumerate(entries):
            u = full_ref[rows(jnp.minimum(block, blocks - 1)), :]
            s = lax.dot_general(u, item_ref[slot], (((1,), (1,)), ((), ())), preferred_element_type=F32)
            w_ref[j] = (conf_ref[tile].astype(F32) * (1.0 - s)).astype(BF16)
        for j, (_, block, slot) in enumerate(entries):
            acc_ref[rows(block - first_block), :] += jnp.dot(w_ref[j], item_ref[slot], preferred_element_type=F32)
        return 0

    lax.fori_loop(0, groups, body, 0)


def fill(item_ref, slot_refs, places):
    tb = item_ref.shape[1]
    for s, ref in zip(places, slot_refs):
        per = ref.shape[0] // tb
        for j in range(per):
            item_ref[s * per + j] = ref[j * tb : (j + 1) * tb, :]


def early(places, count_ref, list_ref, mine_ref, other_ref, conf_ref, _, *refs):
    slot_refs = refs[: len(places)]
    full_ref, acc_ref, item_ref, w_ref = refs[len(places) :]
    half = mine_ref.shape[1]
    here = pl.multiple_of(count_ref[4] * half, half)
    there = pl.multiple_of((1 - count_ref[4]) * half, half)
    full_ref[:, pl.ds(here, half)] = mine_ref[...]
    full_ref[:, pl.ds(there, half)] = other_ref[...]
    fill(item_ref, slot_refs, places)
    run_tiles(0, count_ref[0], 0, list_ref, full_ref, item_ref, conf_ref, w_ref, acc_ref)


def finish(keep_ref, send_ref, acc_ref, scale_ref, fiber, first):
    rows, half = keep_ref.shape
    here = pl.multiple_of(fiber * half, half)
    there = pl.multiple_of((1 - fiber) * half, half)
    scale = scale_ref[first : first + rows, :]
    send_ref[...] = (acc_ref[:rows, pl.ds(there, half)] * scale).astype(BF16)
    keep_ref[...] = acc_ref[:rows, pl.ds(here, half)] * scale


def middle(places, count_ref, list_ref, full_ref, conf_ref, _, __, *refs):
    slot_refs = refs[: len(places)]
    acc_ref, item_ref, w_ref = refs[len(places) :]
    base = list_ref.shape[0] // 4
    fill(item_ref, slot_refs, places)
    run_tiles(base, count_ref[1], 0, list_ref, full_ref, item_ref, conf_ref, w_ref, acc_ref)


def late(places, count_ref, list_ref, full_ref, scale_ref, conf_ref, _, __, *refs):
    slot_refs = refs[: len(places)]
    keep_ref, send_ref, acc_ref, item_ref, w_ref = refs[len(places) :]
    base = list_ref.shape[0] // 4
    fill(item_ref, slot_refs, places)
    run_tiles(2 * base, count_ref[2], 0, list_ref, full_ref, item_ref, conf_ref, w_ref, acc_ref)
    finish(keep_ref, send_ref, acc_ref, scale_ref, count_ref[4], 0)


def second(count_ref, list_ref, full_ref, scale_ref, conf_ref, item_ref, _, __, keep_ref, send_ref, acc_ref, w_ref):
    rows = keep_ref.shape[0]
    base = list_ref.shape[0] // 4
    block = rows // conf_ref.shape[1]
    run_tiles(3 * base, count_ref[3], block, list_ref, full_ref, item_ref, conf_ref, w_ref, acc_ref)
    finish(keep_ref, send_ref, acc_ref, scale_ref, count_ref[4], rows)


def write(part, keep_ref, came_ref, *refs):
    out_ref, buf, sems = refs[-3:]
    rows = keep_ref.shape[0]
    piece = rows // 2
    copies = []
    for i in range(2):
        at = pl.ds(i * piece, piece)
        buf[at, :] = (keep_ref[at, :] + came_ref[at, :].astype(F32)).astype(BF16)
        copies.append(pltpu.make_async_copy(buf.at[at], out_ref.at[pl.ds(part * rows + i * piece, piece)], sems.at[i]))
        copies[-1].start()
    for c in copies:
        c.wait()


def gather_items(items, n_blk):
    def swap(x, bits):
        return lax.ppermute(x, "blk", [(i, i ^ bits) for i in range(n_blk)])

    got = {0: items, 2: swap(items, 2)}
    for d in range(4, n_blk, 4):
        low = d & -d
        got[d] = swap(items if d == low else got[d ^ low], d if d == low else low)
    for d in range(4, n_blk, 4):
        got[d | 2] = swap(got[d], 2)
    for d in range(0, n_blk, 2):
        got[d | 1] = swap(got[d], 1)
    return [got[d] for d in range(n_blk)]


def shards(users, items, tile_users, tile_items, confidence):
    n_fiber, n_blk = lax.axis_size("fiber"), lax.axis_size("blk")
    tb = confidence.shape[-1]
    rows, half = users.shape
    blocks = rows // tb
    per = items.shape[0] // tb
    user_list = tile_users.reshape(-1)
    item_list = tile_items.reshape(-1)
    conf = confidence.reshape(-1, tb, tb)
    tiles = conf.shape[0]
    swap_fiber = [(i, n_fiber - 1 - i) for i in range(n_fiber)]
    other = lax.ppermute(users, "fiber", swap_fiber)
    slots = gather_items(items, n_blk)
    places = ([], [], [])
    for d in range(n_blk):
        chip = d >> 1
        places[0 if chip & (chip - 1) == 0 else 2 if chip == n_blk // 2 - 1 else 1].append(d)
    acc_shape = jax.ShapeDtypeStruct((rows // 2 + tb, 2 * half), F32)
    hbm = [pltpu.with_memory_space_constraint(x, pltpu.HBM) for x in (user_list, item_list, conf, users, items)]
    sums, conf_v, mine, slots[0], order, count, acc, acc2 = pl.pallas_call(
        functools.partial(prepare, n_blk, per, places[1][0]),
        out_shape=(
            jax.ShapeDtypeStruct((blocks, tb), F32),
            jax.ShapeDtypeStruct(conf.shape, BF16),
            jax.ShapeDtypeStruct(users.shape, BF16),
            jax.ShapeDtypeStruct(items.shape, BF16),
            jax.ShapeDtypeStruct((4 * (tiles + STEP),), I32),
            jax.ShapeDtypeStruct((5,), I32),
            acc_shape,
            acc_shape,
        ),
        in_specs=[HBM] * 5,
        out_specs=(VM, VM, VM, VM, SM, SM, VM, VM),
        scratch_shapes=[
            pltpu.SMEM((tiles,), I32),
            pltpu.SMEM((tiles,), I32),
            pltpu.SMEM((n_blk * per,), I32),
            pltpu.SMEM((4,), I32),
            pltpu.VMEM((blocks, tb, tb), F32),
            pltpu.SemaphoreType.DMA((8 + 4,)),
        ],
        compiler_params=params(4),
        cost_estimate=pl.CostEstimate(flops=0, bytes_accessed=conf.size * 4, transcendentals=0),
        name="prepare",
    )(*hbm)
    sums_other = lax.ppermute(sums, "fiber", swap_fiber)
    scale = pl.pallas_call(
        scales,
        out_shape=jax.ShapeDtypeStruct((rows, half), F32),
        in_specs=[VM, VM],
        out_specs=VM,
        compiler_params=params(2),
        name="scales",
    )(sums, sums_other)
    scratch = [pltpu.VMEM((STEP, tb, tb), BF16)]
    gathered = jax.ShapeDtypeStruct((n_blk * per, tb, 2 * half), BF16)
    half_shapes = (jax.ShapeDtypeStruct((rows // 2, half), F32), jax.ShapeDtypeStruct((rows // 2, half), BF16))
    scalars = (count, order)
    full, acc, all_items = pl.pallas_call(
        functools.partial(early, places[0]),
        out_shape=(jax.ShapeDtypeStruct((rows, 2 * half), BF16), acc_shape, gathered),
        in_specs=[SM] * 2 + [VM] * (4 + len(places[0])),
        out_specs=(VM, VM, VM),
        scratch_shapes=scratch,
        input_output_aliases={5: 1},
        compiler_params=params(TILE_MIB),
        cost_estimate=pl.CostEstimate(flops=tiles * tb * tb * half * 8, bytes_accessed=0, transcendentals=0),
        name="early",
    )(*scalars, mine, other, conf_v, acc, *[slots[d] for d in places[0]])
    acc, all_items = pl.pallas_call(
        functools.partial(middle, places[1]),
        out_shape=(acc_shape, gathered),
        in_specs=[SM] * 2 + [VM] * (4 + len(places[1])),
        out_specs=(VM, VM),
        scratch_shapes=scratch,
        input_output_aliases={4: 0, 5: 1},
        compiler_params=params(TILE_MIB),
        cost_estimate=pl.CostEstimate(flops=tiles * tb * tb * half * 4, bytes_accessed=0, transcendentals=0),
        name="middle",
    )(*scalars, full, conf_v, acc, all_items, *[slots[d] for d in places[1]])
    keep, send, _, all_items = pl.pallas_call(
        functools.partial(late, places[2]),
        out_shape=(*half_shapes, acc_shape, gathered),
        in_specs=[SM] * 2 + [VM] * (5 + len(places[2])),
        out_specs=(VM, VM, VM, VM),
        scratch_shapes=scratch,
        input_output_aliases={5: 2, 6: 3},
        compiler_params=params(TILE_MIB),
        cost_estimate=pl.CostEstimate(flops=tiles * tb * tb * half * 8, bytes_accessed=0, transcendentals=0),
        name="late",
    )(*scalars, full, scale, conf_v, acc, all_items, *[slots[d] for d in places[2]])
    arrived = lax.ppermute(send, "fiber", swap_fiber)
    keep2, send2, _ = pl.pallas_call(
        second,
        out_shape=(*half_shapes, acc_shape),
        in_specs=[SM] * 2 + [VM] * 6,
        out_specs=(VM, VM, VM),
        scratch_shapes=scratch,
        input_output_aliases={6: 2},
        compiler_params=params(TILE_MIB),
        cost_estimate=pl.CostEstimate(flops=tiles * tb * tb * half * 8, bytes_accessed=0, transcendentals=0),
        name="second",
    )(*scalars, full, scale, conf_v, all_items, acc2, keep)
    arrived2 = lax.ppermute(send2, "fiber", swap_fiber)
    out = None
    for i, (kept, came) in enumerate(((keep, arrived), (keep2, arrived2))):
        out = pl.pallas_call(
            functools.partial(write, i),
            out_shape=pltpu.HBM(users.shape, BF16),
            in_specs=[VM, VM] + [HBM] * i,
            out_specs=HBM,
            scratch_shapes=[pltpu.VMEM(came.shape, BF16), pltpu.SemaphoreType.DMA((2,))],
            input_output_aliases={2: 0} if i else {},
            compiler_params=params(2),
        )(kept, came, *([out] if i else []))
    return out


def solution(mesh):
    in_specs = (
        P("blk", "fiber"),
        P("blk", None),
        P("blk", "fiber", None),
        P("blk", "fiber", None),
        P("blk", "fiber", None, None, None),
    )
    return jax.shard_map(shards, mesh=mesh, in_specs=in_specs, out_specs=P("blk", "fiber"), check_vma=False)
```
